32 devices in a mesh: groups: 2 (over x), ctx: 16 (over z, y, core).
Axes of the slice: x: 2, y: 2, z: 4, core: 2. Of those that a mesh axis runs over, the one named last changes fastest.
Arguments:
- q_span: bfloat16 [2048, 8192], P(('groups', 'ctx')), parts along dimension 0, may hold values from -200 to 200
- k_span: bfloat16 [2048, 1024], P(('groups', 'ctx')), parts along dimension 0, may hold values from -30 to 30
- v_span: bfloat16 [2048, 1024], P(('groups', 'ctx')), parts along dimension 0, may hold values from -6 to 6
- k_prefix: bfloat16 [1024, 1024], P(('groups', 'ctx')), parts along dimension 0, may hold values from -30 to 30
- v_prefix: bfloat16 [1024, 1024], P(('groups', 'ctx')), parts along dimension 0, may hold values from -6 to 6
- start_offset: int32 [2], P('groups'), parts along dimension 0, may hold values from 0 to 511
- prefix_len: int32 [2], P('groups'), parts along dimension 0, may hold values from 1 to 512
- block_order: int32 [64], P('groups'), parts along dimension 0, may hold values from 0 to 31, each once
Outputs:
- attended: bfloat16 [2048, 8192], P(('groups', 'ctx')), parts along dimension 0
The draws below stay inside these ranges and needn't reach their ends.
There are 2 independent parts, one for each index of `groups`. The reference program is written for one: setup_inputs(seed, part) draws one part's arguments, and reference() takes and returns one part's arrays. A program takes and returns all parts, laid end to end along the dimension named above; each array names one. Nothing has to cross between parts.
All inputs are finite; a program needn't handle non-finite values.
Results may differ from the reference program's by a relative error of at most 0.006.
Values may be sent and summed in bfloat16 or wider, within the bound.
No kernel may reach another device: no remote copies, remote signals or barrier semaphores. Data moves between devices by JAX's collectives and lax.ppermute only.
A program may use at most 128 MiB of HBM per device.

```python
import math
import jax
import jax.numpy as jnp
from jax import lax

HQ = 64
KVH = 8
HD = 128
C_DEV = 64
SPAN = 1024
PREFIX = 512
N_CTX = 16


def draw_q_span(key, part):
    base = jnp.clip(jax.random.normal(jax.random.fold_in(key, 21), (SPAN, HQ * HD), jnp.float32), -6.0, 6.0)
    return base.astype(jnp.bfloat16)


def draw_k_span(key, part):
    base = jnp.clip(jax.random.normal(jax.random.fold_in(key, 22), (SPAN, KVH * HD), jnp.float32), -6.0, 6.0)
    return base.astype(jnp.bfloat16)


def draw_k_prefix(key, part):
    base = jnp.clip(jax.random.normal(jax.random.fold_in(key, 23), (PREFIX, KVH * HD), jnp.float32), -6.0, 6.0)
    return base.astype(jnp.bfloat16)


def levels(stream_key, extent, shards, low, high):
    def one(position, shards_of):
        steps = jax.random.uniform(jax.random.fold_in(jax.random.fold_in(stream_key, 6), position), (shards_of,), jnp.float32, low / len(shards), high / len(shards))
        return jnp.repeat(jnp.exp(steps), extent[position] // shards_of).reshape((-1,) + (1,) * (len(extent) - position - 1))

    gain = one(*shards[0])
    for cut in shards[1:]:
        gain = gain * one(*cut)
    return gain


def gaussian(own_key, dims, deviation, most, pieces=(), kind=jnp.bfloat16):
    level = levels(own_key, dims, pieces, -0.22, 0.18) if pieces else 1.0
    drawn = jax.random.normal(own_key, dims, jnp.float32) * deviation * level
    return jnp.minimum(jnp.maximum(drawn, -most), most).astype(kind)


def setup_inputs(seed: int = 0, part: int = 0) -> dict:
    key_list = jax.random.split(jax.random.key(seed), 9)
    own_keys = jax.random.split(jax.random.fold_in(key_list[8], part), 9)
    q_span = draw_q_span(jax.random.fold_in(jax.random.fold_in(key_list[8], part), 71), part)
    k_span = draw_k_span(jax.random.fold_in(jax.random.fold_in(key_list[8], part), 71), part)
    v_span = gaussian(own_keys[2], (SPAN, KVH * HD), 1.0, 6.0, ((0, 16),))
    k_prefix = draw_k_prefix(jax.random.fold_in(jax.random.fold_in(key_list[8], part), 71), part)
    v_prefix = gaussian(own_keys[4], (PREFIX, KVH * HD), 1.0, 6.0, ((0, 16),))
    start_offset = jax.random.randint(own_keys[5], (1,), 0, SPAN // 2).astype(jnp.int32)
    prefix_len = jax.random.randint(own_keys[6], (1,), 1, PREFIX + 1).astype(jnp.int32)
    block_order = jax.random.permutation(own_keys[7], 2 * N_CTX).astype(jnp.int32)
    return {"q_span": q_span, "k_span": k_span, "v_span": v_span, "k_prefix": k_prefix, "v_prefix": v_prefix, "start_offset": start_offset, "prefix_len": prefix_len, "block_order": block_order}


def reference(q_span, k_span, v_span, k_prefix, v_prefix, start_offset, prefix_len, block_order):
    total_rows = q_span.shape[0]
    block_rows = C_DEV // 2
    per_group = HQ // KVH
    row_ids = jnp.arange(total_rows, dtype=jnp.int32)
    positions = (block_order[row_ids // block_rows] * block_rows + row_ids % block_rows).astype(jnp.int32)
    prefix_ids = jnp.arange(k_prefix.shape[0], dtype=jnp.int32)
    prefix_ok = prefix_ids < prefix_len[0]
    key_all = jnp.concatenate([k_prefix, k_span], 0).astype(jnp.float32).reshape(-1, KVH, HD)
    value_all = jnp.concatenate([v_prefix, v_span], 0).astype(jnp.float32).reshape(-1, KVH, HD)
    scaling = 1.0 / math.sqrt(HD)
    query_block = math.gcd(total_rows, 128)
    count = total_rows // query_block
    query_blocks = q_span.reshape(count, query_block, KVH, per_group, HD)
    pos_blocks = positions.reshape(count, query_block)

    def one_block(packed):
        query_rows, query_pos = packed
        scores = jnp.einsum('qhgd,khd->hgqk', query_rows.astype(jnp.float32), key_all) * scaling
        causal = (positions[None, :] <= query_pos[:, None]) & (positions[None, :] >= start_offset[0])
        visible = jnp.concatenate([jnp.broadcast_to(prefix_ok[None, :], (query_block, prefix_ids.shape[0])), causal], 1)
        scores = jnp.where(visible[None, None], scores, jnp.float32(-1e+30))
        largest = lax.optimization_barrier(jnp.max(scores, axis=-1, keepdims=True))
        weights = jnp.where(visible[None, None], jnp.exp(scores - largest), jnp.float32(0.0))
        total = lax.optimization_barrier(jnp.sum(weights, axis=-1))
        rounded = lax.optimization_barrier(weights.astype(jnp.bfloat16)).astype(jnp.float32)
        summed = jnp.einsum('hgqk,khd->hgqd', rounded, value_all)
        result = summed / total[..., None]
        return result.transpose(2, 0, 1, 3).reshape(query_block, HQ * HD)
    outputs = lax.map(one_block, (query_blocks, pos_blocks))
    return outputs.reshape(total_rows, HQ * HD).astype(jnp.bfloat16)
```

```python
import functools
import math

import jax
import jax.numpy as jnp
from jax import lax
from jax.experimental import pallas as pl
from jax.experimental.pallas import tpu as pltpu
from jax.sharding import PartitionSpec as P

HD = 128
MASKED = -1e30
NEVER = 1 << 30


def chip_ring(mesh):
    names = list(mesh.axis_names)
    line = mesh.devices.transpose([names.index("ctx")] + [i for i, n in enumerate(names) if n != "ctx"])
    line = line.reshape(line.shape[0], -1)[::2, 0]
    natural = list(range(len(line)))
    if not all(hasattr(d, "coords") for d in line):
        return natural
    coords = [tuple(d.coords) for d in line]
    axes = [a for a in range(len(coords[0])) if len({c[a] for c in coords}) > 1]
    if len(axes) == 2:
        for narrow, wide in (axes, axes[::-1]):
            columns = sorted({c[narrow] for c in coords})
            if len(columns) == 2:
                up = sorted((i for i in natural if coords[i][narrow] == columns[0]), key=lambda i: coords[i][wide])
                down = sorted((i for i in natural if coords[i][narrow] == columns[1]), key=lambda i: -coords[i][wide])
                return up + down
    return natural


def attend_kernel(n_pieces, span_rows, first, last, coef, c_ref, *refs):
    q_mine, q_other, kpos, qpos = refs[:4]
    pieces = refs[4 : 4 + n_pieces]
    rest = refs[4 + n_pieces :]
    if not first:
        m_in, l_in, a_in = rest[:3]
        rest = rest[3:]
    if last:
        out_mine, out_other, bias = rest
    else:
        m_out, l_out, a_out, bias = rest
    rows = q_mine.shape[0]
    heads = q_mine.shape[1] // HD
    keys_piece = pieces[0].shape[0] // 2

    @pl.when(pl.program_id(0) == 0)
    def _():
        bias[...] = jnp.where(kpos[...] <= qpos[...], 0.0, MASKED)

    k = jnp.concatenate([p[:keys_piece, :] for p in pieces], axis=0)
    v = jnp.concatenate([p[keys_piece:, :] for p in pieces], axis=0)
    v = jnp.concatenate([v, jnp.ones_like(v)], axis=1)
    for h in range(heads):
        at = slice(h * HD, (h + 1) * HD)
        block = slice(h * 2 * rows, (h + 1) * 2 * rows)
        q = jnp.concatenate([q_mine[:, at], q_other[:, at]], axis=0)
        s = lax.dot_general(q, k, (((1,), (1,)), ((), ())), preferred_element_type=jnp.float32)
        s = s + bias[...]
        m = jnp.max(s, axis=1, keepdims=True)
        if not first:
            m_old = m_in[block, :]
            m_wide = jnp.maximum(m_old, m)
            m = m_wide[:, :1]
            scale = jnp.exp2((m_old - m_wide) * coef)
        w = jnp.exp2((s - m) * coef).astype(jnp.bfloat16)
        pv = jnp.dot(w, v, preferred_element_type=jnp.float32)
        acc, total = pv[:, :HD], pv[:, HD:]
        if not first:
            acc = acc + a_in[block, :] * scale
            total = total + l_in[block, :] * scale
        if last:
            o = (acc / total).astype(jnp.bfloat16)
            out_mine[:, at] = o[:rows]
            out_other[:, at] = o[rows:]
        else:
            m_out[block, :] = jnp.broadcast_to(m, (2 * rows, HD)) if first else m_wide
            l_out[block, :] = total
            a_out[block, :] = acc


def attend(core, q_mine, q_other, kpos, qpos, pieces, state, last, coef):
    rows, q_half = q_other.shape
    heads_here = pieces[0].shape[1] // HD
    width = q_half // heads_here
    keys = kpos.shape[1]
    first = state is None
    q_rows = 2 * rows * (width // HD)
    piece_rows = pieces[0].shape[0]
    state_spec = pl.BlockSpec((q_rows, HD), lambda g, c: (g, 0))
    in_specs = [
        pl.BlockSpec((rows, width), lambda g, c: (0, c[0] * heads_here + g)),
        pl.BlockSpec((rows, width), lambda g, c: (0, g)),
        pl.BlockSpec((1, keys), lambda g, c: (0, 0)),
        pl.BlockSpec((2 * rows, 1), lambda g, c: (0, 0)),
    ] + [pl.BlockSpec((piece_rows, HD), lambda g, c: (0, g))] * len(pieces)
    args = [core, q_mine, q_other, kpos, qpos, *pieces]
    aliases = {}
    if not first:
        if not last:
            aliases = {len(args) + i: i for i in range(3)}
        args += list(state)
        in_specs += [state_spec] * 3
    if last:
        out_shape = (
            jax.ShapeDtypeStruct(q_mine.shape, jnp.bfloat16),
            jax.ShapeDtypeStruct(q_other.shape, jnp.bfloat16),
        )
        out_specs = (
            pl.BlockSpec((rows, width), lambda g, c: (0, c[0] * heads_here + g)),
            pl.BlockSpec((rows, width), lambda g, c: (0, g)),
        )
    else:
        out_shape = (jax.ShapeDtypeStruct((q_rows * heads_here, HD), jnp.float32),) * 3
        out_specs = (state_spec,) * 3
    total_rows = q_rows * heads_here
    return pl.pallas_call(
        functools.partial(attend_kernel, len(pieces), rows, first, last, coef),
        grid_spec=pltpu.PrefetchScalarGridSpec(
            num_scalar_prefetch=1,
            grid=(heads_here,),
            in_specs=in_specs,
            out_specs=out_specs,
            scratch_shapes=[pltpu.VMEM((2 * rows, keys), jnp.float32)],
        ),
        out_shape=out_shape,
        input_output_aliases=aliases,
        compiler_params=pltpu.CompilerParams(vmem_limit_bytes=24 << 20),
        cost_estimate=pl.CostEstimate(
            flops=4 * total_rows * keys * HD,
            bytes_accessed=4 * total_rows * HD * 4,
            transcendentals=total_rows * keys,
        ),
    )(*args)


def place_kernel(c_ref, got, whole, out):
    out[...] = got[...]


def place(core, got, whole):
    rows, width = got.shape
    return pl.pallas_call(
        place_kernel,
        grid_spec=pltpu.PrefetchScalarGridSpec(
            num_scalar_prefetch=1,
            grid=(1,),
            in_specs=[
                pl.BlockSpec((rows, width), lambda g, c: (0, 0)),
                pl.BlockSpec(memory_space=pl.ANY),
            ],
            out_specs=pl.BlockSpec((rows, width), lambda g, c: (0, 1 - c[0])),
        ),
        out_shape=jax.ShapeDtypeStruct(whole.shape, whole.dtype),
        input_output_aliases={2: 0},
        compiler_params=pltpu.CompilerParams(vmem_limit_bytes=8 << 20),
    )(core, got, whole)


def make_local(ring):
    chips = len(ring)
    place_of = {chip: i for i, chip in enumerate(ring)}

    def pairs(shift, cross):
        return [
            (2 * chip + c, 2 * ring[(place_of[chip] + shift) % chips] + (c ^ cross))
            for chip in range(chips)
            for c in range(2)
        ]

    def send(x, shift, cross=0):
        return lax.ppermute(x, "ctx", pairs(shift, cross))

    shifts = [0] + [s for step in range(1, chips // 2) for s in (step, -step)] + [chips // 2]
    arrivals = [
        [2 * ring[(place_of[d // 2] - s) % chips] + (d % 2 ^ cross) for s in shifts for cross in (0, 1)]
        for d in range(2 * chips)
    ]

    def local(q_span, k_span, v_span, k_prefix, v_prefix, start_offset, prefix_len, block_order):
        rows, q_width = q_span.shape
        block = rows // 2
        prefix_rows = k_prefix.shape[0]
        kv_width = k_span.shape[1]
        members = 2 * chips
        me = lax.axis_index("ctx")
        core = me % 2
        coef = 1.0 / math.sqrt(HD) * math.log2(math.e)

        kv = jnp.concatenate([k_span, k_prefix, v_span, v_prefix], axis=0)
        mine = lax.dynamic_slice_in_dim(kv, core * (kv_width // 2), kv_width // 2, 1)
        theirs = lax.dynamic_slice_in_dim(kv, (1 - core) * (kv_width // 2), kv_width // 2, 1)
        q_theirs = lax.dynamic_slice_in_dim(q_span, (1 - core) * (q_width // 2), q_width // 2, 1)

        span_pos = jnp.repeat(block_order.reshape(members, 2), block, axis=1) * block + jnp.tile(
            jnp.arange(block, dtype=jnp.int32), 2
        )
        span_key = jnp.where(span_pos >= start_offset[0], span_pos, NEVER)
        prefix_id = jnp.arange(members * prefix_rows, dtype=jnp.int32).reshape(members, prefix_rows)
        prefix_key = jnp.where(prefix_id < prefix_len[0], -1, NEVER)
        key_pos = jnp.concatenate([span_key, prefix_key], axis=1)
        order = jnp.asarray(arrivals, jnp.int32)[me]
        picked = order[:, None] == jnp.arange(members, dtype=jnp.int32)[None, :]
        key_pos = jnp.sum(jnp.where(picked[:, :, None], key_pos[None], 0), axis=1)
        query_pos = jnp.sum(jnp.where(picked[:2, :, None], span_pos[None], 0), axis=1).reshape(2 * rows, 1)
        core_arr = core.astype(jnp.int32).reshape(1)

        own = [mine, send(theirs, 0, 1)]
        q_other = send(q_theirs, 0, 1)
        ahead = [send(mine, 1), send(theirs, 1, 1)]
        behind = [send(mine, -1), send(theirs, -1, 1)]
        groups = [own + ahead + behind]
        for _ in range(chips // 2 - 2):
            ahead = [send(x, 1) for x in ahead]
            behind = [send(x, -1) for x in behind]
            groups.append(ahead + behind)
        groups.append([send(ahead[0], 1), send(behind[1], -1)])

        state = None
        at = 0
        for i, pieces in enumerate(groups):
            n = len(pieces)
            kpos = key_pos[at : at + n].reshape(1, -1)
            at += n
            last = i == len(groups) - 1
            state = attend(core_arr, q_span, q_other, kpos, query_pos, pieces, state, last, coef)
        out, out_theirs = state
        return place(core_arr, send(out_theirs, 0, 1), out)

    return local


def solution(mesh):
    split = P(("groups", "ctx"), None)
    placed = (split,) * 5 + (P("groups"),) * 3
    return jax.shard_map(
        make_local(chip_ring(mesh)), mesh=mesh, in_specs=placed, out_specs=split, check_vma=False
    )
```
